128 devices in a mesh: gx: 16 (over y, z), gy: 8 (over x, core).
Axes of the slice: x: 4, y: 4, z: 4, core: 2. Of those that a mesh axis runs over, the one named last changes fastest.
Arguments:
- points: bfloat16 [1024, 128, 512], P(('gx', 'gy')), may hold values from -6 to 6
- moved_to: int32 [2, 2, 1024], P(None, None, ('gx', 'gy')), may hold values from 0 to 1023, as said below
- gains: float32 [2, 2, 512], replicated, may hold values from 0.1 to 1.9
- w_qkv: bfloat16 [2, 512, 1536], replicated, may hold values from -4 to 4
- w_out: bfloat16 [2, 512, 512], replicated, may hold values from -0.25 to 0.25
- w_up: bfloat16 [2, 512, 2048], replicated, may hold values from -0.25 to 0.25
- w_down: bfloat16 [2, 2048, 512], replicated, may hold values from -0.125 to 0.125
Outputs:
- encoded: bfloat16 [1024, 128, 512], P(('gx', 'gy'))
The draws below stay inside these ranges and needn't reach their ends.
Inputs may be any that keep to these rules, and one draw needn't show every extreme that they name: Each moved_to[l, s] is a permutation of the 1024 positions. The owner of position p is p // 8, with owner index = gx index * 8 + gy index. Section 0 keeps every brick's gy index, section 1 its gx index. From one owner at most 2 bricks go to any one owner in section 0 and at most 2 in section 1; in every layer, section and group some owner sends exactly that many to one owner.
All inputs are finite; a program needn't handle non-finite values.
Results may differ from the reference program's by a relative error of at most 0.018.
Values may be sent and summed in bfloat16 or wider, within the bound.
A program may use at most 128 MiB of HBM per device.

```python
import math
import jax
import jax.numpy as jnp
from jax import lax

D = 512
FF = 2048
HEAD_DIM = 16
BRICK = 128
PATCH = 512
LAYERS = 2
BR_DEV = 8
BRICKS = 1024
N_GX = 16
N_GY = 8


def many_perms(key, count, length):
    return jax.vmap(lambda single: jax.random.permutation(single, length))(jax.random.split(key, count))


def section_targets(key, groups, peers, br):
    cap = max(2, -(-br // peers))
    split_keys = jax.random.split(key, 5)
    rotate = many_perms(split_keys[0], groups, peers)
    relabel = many_perms(split_keys[1], groups, peers)
    offsets = many_perms(split_keys[2], groups, peers)
    slots = jnp.arange(br)
    pick = jnp.where(slots < cap, 0, 1 + (slots - cap) % (peers - 1))
    offset_slot = offsets[:, pick]
    slot_of = many_perms(split_keys[3], groups * peers, br).reshape(groups, peers, br)
    place_of = many_perms(split_keys[4], groups * peers, br).reshape(groups, peers, br)
    offset_at = jnp.take_along_axis(jnp.broadcast_to(offset_slot[:, None, :], (groups, peers, br)), slot_of, axis=2)
    circle = (rotate[:, :, None] + offset_at) % peers
    target = jnp.take_along_axis(jnp.broadcast_to(relabel[:, None, :], (groups, peers, peers)), circle, axis=2)
    group_index = jnp.arange(groups)[:, None, None]
    position = place_of[group_index, target, slot_of]
    return (target, position)


def draw_moved_to(key, part):
    layers_out = []
    for layer in range(LAYERS):
        row_key = jax.random.fold_in(jax.random.fold_in(key, 101), layer)
        col_key = jax.random.fold_in(jax.random.fold_in(key, 202), layer)
        target, position = section_targets(row_key, N_GY, N_GX, BR_DEV)
        column = jnp.arange(N_GY)[:, None, None]
        first = ((target * N_GY + column) * BR_DEV + position).transpose(1, 0, 2).reshape(-1)
        target, position = section_targets(col_key, N_GX, N_GY, BR_DEV)
        row = jnp.arange(N_GX)[:, None, None]
        second = ((row * N_GY + target) * BR_DEV + position).reshape(-1)
        layers_out.append(jnp.stack([first, second]))
    return jnp.stack(layers_out).astype(jnp.int32)


def draw_w_qkv(key, part):
    base = jax.random.normal(key, (LAYERS, D, 3 * D), jnp.float32) * (1.0 / jnp.sqrt(jnp.float32(D)))
    return jnp.clip(base, -4.0, 4.0).astype(jnp.bfloat16)


def block_scale(rng, extent, cuts, low, top_value):
    factor_of = 1.0
    for dim, blocks in cuts:
        heights = jax.random.uniform(jax.random.fold_in(jax.random.fold_in(rng, 6), dim), (blocks,), jnp.float32, low / len(cuts), top_value / len(cuts))
        factor_of = factor_of * jnp.repeat(jnp.exp(heights), extent[dim] // blocks).reshape((-1,) + (1,) * (len(extent) - 1 - dim))
    return factor_of


def scatter_about(stream_key, extent, scale, reach, cuts=(), kind=jnp.bfloat16):
    level = block_scale(stream_key, extent, cuts, -0.22, 0.18) if cuts else 1.0
    array = jax.random.normal(stream_key, extent, jnp.float32) * scale * level
    return jnp.minimum(jnp.maximum(array, -reach), reach).astype(kind)


def setup_inputs(seed: int = 0) -> dict:
    key_list = jax.random.split(jax.random.key(seed), 8)
    return {
        "points": scatter_about(key_list[0], (BRICKS, BRICK, D), 1.0, 6.0, ((0, 128),)),
        "moved_to": draw_moved_to(jax.random.fold_in(key_list[7], 71), 0),
        "gains": jnp.clip(1.0 + 0.18 * jax.random.normal(key_list[2], (LAYERS, 2, D), jnp.float32), 0.1, 1.9),
        "w_qkv": draw_w_qkv(jax.random.fold_in(key_list[7], 71), 0),
        "w_out": scatter_about(key_list[4], (LAYERS, D, D), D ** -0.5, 0.25),
        "w_up": scatter_about(key_list[5], (LAYERS, D, FF), D ** -0.5, 0.25),
        "w_down": scatter_about(key_list[6], (LAYERS, FF, D), FF ** -0.5, 0.125),
    }


def normalize(values, gain):
    values = values.astype(jnp.float32)
    center = values - lax.optimization_barrier(jnp.mean(values, axis=1, keepdims=True))
    spread = lax.optimization_barrier(jnp.mean(center * center, axis=1, keepdims=True))
    return center * lax.rsqrt(spread + 1e-05) * gain

def attend_patch(patch):
    width = patch.shape[1] // 3
    count = patch.shape[0]
    heads = width // HEAD_DIM
    block = min(8, heads)
    scale = 1.0 / math.sqrt(HEAD_DIM)
    query = patch[:, :width].reshape(count, heads, HEAD_DIM).astype(jnp.float32)
    keys = patch[:, width:2 * width].reshape(count, heads, HEAD_DIM).astype(jnp.float32)
    values = patch[:, 2 * width:].reshape(count, heads, HEAD_DIM).astype(jnp.float32)
    pieces = []
    for first in range(0, heads, block):
        scores = jnp.einsum('qhd,khd->hqk', query[:, first:first + block], keys[:, first:first + block]) * scale
        peak = lax.optimization_barrier(jnp.max(scores, axis=2, keepdims=True))
        weights = jnp.exp(scores - peak)
        probs = (weights / lax.optimization_barrier(jnp.sum(weights, axis=2, keepdims=True))).astype(jnp.bfloat16)
        mixed = jnp.einsum('hqk,khd->qhd', probs.astype(jnp.float32), values[:, first:first + block])
        pieces.append(mixed.reshape(count, block * HEAD_DIM))
    return jnp.concatenate(pieces, axis=1).astype(jnp.bfloat16)

def encoder_layer(bricks, gain, w_qkv, w_out, w_up, w_down):
    shape = bricks.shape
    flat = bricks.reshape(-1, shape[2])
    normed = normalize(flat, gain[0]).astype(jnp.bfloat16)
    projected = jnp.dot(normed, w_qkv, preferred_element_type=jnp.float32).astype(jnp.bfloat16)
    attended = lax.map(attend_patch, projected.reshape(-1, PATCH, projected.shape[1])).reshape(flat.shape)
    mixed = (flat.astype(jnp.float32) + jnp.dot(attended, w_out, preferred_element_type=jnp.float32)).astype(jnp.bfloat16)
    inner = normalize(mixed, gain[1]).astype(jnp.bfloat16)
    hidden = jax.nn.gelu(jnp.dot(inner, w_up, preferred_element_type=jnp.float32), approximate=False).astype(jnp.bfloat16)
    result = mixed.astype(jnp.float32) + jnp.dot(hidden, w_down, preferred_element_type=jnp.float32)
    return result.astype(jnp.bfloat16).reshape(shape)

def reference(points, moved_to, gains, w_qkv, w_out, w_up, w_down):
    bricks = points
    for layer in range(LAYERS):
        for section in range(2):
            bricks = jnp.zeros_like(bricks).at[moved_to[layer, section]].set(bricks)
        bricks = encoder_layer(bricks, gains[layer], w_qkv[layer], w_out[layer], w_up[layer], w_down[layer])
    return bricks
```

```python
import functools
import math

import jax
import jax.numpy as jnp
from jax import lax
from jax.experimental import pallas as pl
from jax.experimental.pallas import tpu as pltpu
from jax.sharding import PartitionSpec as P

MESH = pl.DeviceIdType.MESH
F32 = jnp.float32
BF16 = jnp.bfloat16

LAYERS = 2
DEVICES = 128
GY = 8
D = 512
FF = 2048
FF_BLOCK = 512
HEAD_DIM = 16
PATCH = 512
GROUP = 128
HEADS = GROUP // HEAD_DIM
HALF = D // 2
ROWS = 2048
SCALE = math.log2(math.e) / math.sqrt(HEAD_DIM)


def iota(shape, dim):
    return lax.broadcasted_iota(jnp.int32, shape, dim)


def dot(a, b):
    return jnp.dot(a, b, preferred_element_type=F32)


def one_hot(hit):
    return jnp.where(hit, 1.0, 0.0).astype(BF16)


def row_norm(values, gain):
    center = values - jnp.mean(values, axis=1, keepdims=True)
    spread = jnp.mean(center * center, axis=1, keepdims=True)
    return center * lax.rsqrt(spread + 1e-05) * gain


def local_row(canonical):
    return (canonical % 4) * 128 + (canonical // 8) * 2 + (canonical // 4) % 2


def kernel(
    x_ref, moved_ref, gains_ref, qkv_hbm, out_hbm, up_hbm, down_hbm, o_ref,
    w_qkv, w_out, w_up, w_down, stage, mid, spread, final, table, order, qkv, probs, blocks, attended,
    weight_sem, local_sem, table_sems, send1, recv1, send2, recv2,
):
    me = lax.axis_index("gx") * GY + lax.axis_index("gy")

    def place(device):
        return (device // GY, device % GY)

    def each_peer(body):
        def step(i, carry):
            body((me + i) % DEVICES)
            return carry

        lax.fori_loop(1, DEVICES, step, 0)

    weights = []
    for i, (src, dst) in enumerate(
        ((qkv_hbm, w_qkv), (out_hbm, w_out), (up_hbm, w_up), (down_hbm, w_down))
    ):
        copy = pltpu.make_async_copy(src, dst, weight_sem.at[i])
        copy.start()
        weights.append(copy)

    barrier = pltpu.get_barrier_semaphore()
    each_peer(
        lambda p: pl.semaphore_signal(barrier, inc=1, device_id=place(p), device_id_type=MESH)
    )

    to_canonical = one_hot(
        iota((PATCH, PATCH), 1) == local_row(iota((PATCH, PATCH), 0))
    )
    for a in range(2):
        rows = dot(to_canonical, x_ref[a * PATCH : (a + 1) * PATCH, :])
        for h in range(2):
            stage[0, a, h] = rows[:, h * HALF : (h + 1) * HALF].reshape(64, 8, HALF).astype(BF16)
    table[me] = moved_ref[...]

    pl.semaphore_wait(barrier, DEVICES - 1)

    def send_table(p):
        pltpu.make_async_remote_copy(
            src_ref=moved_ref, dst_ref=table.at[me], send_sem=table_sems.at[0],
            recv_sem=table_sems.at[1], device_id=place(p), device_id_type=MESH,
        ).start()

    def send_spread(layer, a):
        def send(p):
            pltpu.make_async_remote_copy(
                src_ref=stage.at[layer, a, p % 2, p // 2], dst_ref=spread.at[layer, a, me],
                send_sem=send1.at[layer, a], recv_sem=recv1.at[layer, a],
                device_id=place(p), device_id_type=MESH,
            ).start()

        each_peer(send)
        own = pltpu.make_async_copy(
            stage.at[layer, a, me % 2, me // 2], spread.at[layer, a, me], local_sem
        )
        own.start()
        own.wait()

    def send_final(layer, a):
        def send(p):
            pltpu.make_async_remote_copy(
                src_ref=mid.at[layer, a, p], dst_ref=final.at[layer, a, me % 2, me // 2],
                send_sem=send2.at[layer, a], recv_sem=recv2.at[layer, a],
                device_id=place(p), device_id_type=MESH,
            ).start()

        each_peer(send)
        own = pltpu.make_async_copy(
            mid.at[layer, a, me], final.at[layer, a, me % 2, me // 2], local_sem
        )
        own.start()
        own.wait()

    def await_bytes(layer, a, sem):
        part = spread.at[layer, a, 0 : DEVICES - 1]
        pltpu.make_async_copy(part, part, sem.at[layer, a]).wait()

    each_peer(send_table)
    for a in range(2):
        send_spread(0, a)

    head_of = iota((PATCH, GROUP), 1) // HEAD_DIM
    for h in range(HEADS):
        blocks[h * PATCH : (h + 1) * PATCH, GROUP:] = one_hot(head_of == h)

    part = table.at[0 : DEVICES - 1]
    pltpu.make_async_copy(part, part, table_sems.at[1]).wait()
    pltpu.make_async_copy(part, part, table_sems.at[0]).wait()
    moves = table[...].reshape(DEVICES, DEVICES).astype(F32).T[0:32]
    high = jnp.floor(moves * (1 / 32))
    low = (moves - high * 32).astype(BF16)
    high = high.astype(BF16)

    def along(width, owner, slot):
        owners = one_hot(iota((DEVICES, width), 0) == owner(iota((DEVICES, width), 1)))
        hit = iota((32, width), 0) % 8 == slot(iota((32, width), 1))
        both = [jnp.where(hit, dot(v, owners), 0.0) for v in (high, low)]
        return lambda i: [
            jnp.sum(v[i * 8 : (i + 1) * 8], axis=0, keepdims=True) for v in both
        ]

    by_row = along(ROWS, lambda i: i // 8 % DEVICES, lambda i: i // 1024 * 4 + i % 4)
    by_brick = along(1024, lambda i: i // 8, lambda i: i % 8)
    for layer in range(LAYERS):
        first = by_row(2 * layer)
        first = first[0] * 32 + first[1]
        second = by_brick(2 * layer + 1)
        hit = one_hot(iota((1024, ROWS), 0).astype(F32) == first)
        both = jnp.concatenate(second, axis=0).astype(BF16)
        both = dot(jnp.concatenate([both] * 4, axis=0), hit)
        point = (iota((1, ROWS), 1) // 4 % 2).astype(F32)
        code = (both[0:1] * 32 + both[1:2]) * 2 + point
        for r in range(0, ROWS, 512):
            p = iota((512, 1), 0) + r
            want = (p // 8 % DEVICES * 8 + p // 1024 * 4 + p % 4) * 2 + p // 4 % 2
            order[layer, r : r + 512, :] = one_hot(want.astype(F32) == code)

    for copy in weights:
        copy.wait()

    def encode(layer, a):
        x = jnp.concatenate(
            [final[layer, a, h].astype(F32).reshape(PATCH, HALF) for h in range(2)], axis=1
        )
        normed = row_norm(x, gains_ref[layer, 0:1, :]).astype(BF16)
        qkv[:, 0:D] = (dot(normed, w_qkv[layer, :, 0:D]) * SCALE).astype(BF16)
        qkv[:, D:] = dot(normed, w_qkv[layer, :, D:]).astype(BF16)

        def group(g, carry):
            off = pl.multiple_of(g * GROUP, GROUP)
            query = qkv[:, pl.ds(off, GROUP)]
            keys = qkv[:, pl.ds(pl.multiple_of(D + off, GROUP), GROUP)]
            values = qkv[:, pl.ds(pl.multiple_of(2 * D + off, GROUP), GROUP)]
            zero = jnp.zeros((), BF16)
            for h in range(HEADS):
                rows = slice(h * PATCH, (h + 1) * PATCH)
                blocks[rows, 0:GROUP] = jnp.where(head_of == h, values, zero)
                scores = lax.dot_general(
                    jnp.where(head_of == h, query, zero), keys, (((1,), (1,)), ((), ())),
                    preferred_element_type=F32,
                )
                peak = jnp.max(scores, axis=1, keepdims=True)
                probs[:, rows] = jnp.exp2(scores - peak).astype(BF16)
            mixed = dot(probs[...], blocks[...])
            attended[:, pl.ds(off, GROUP)] = (mixed[:, 0:GROUP] / mixed[:, GROUP:]).astype(BF16)
            return carry

        lax.fori_loop(0, D // GROUP, group, 0)
        mixed = (x + dot(attended[...], w_out[layer])).astype(BF16).astype(F32)
        inner = row_norm(mixed, gains_ref[layer, 1:2, :]).astype(BF16)
        result = mixed
        for c in range(0, FF, FF_BLOCK):
            up = dot(inner, w_up[layer, :, c : c + FF_BLOCK])
            hidden = (0.5 * up * (1.0 + lax.erf(up * math.sqrt(0.5)))).astype(BF16)
            result = result + dot(hidden, w_down[layer, c : c + FF_BLOCK, :])
        return result

    def run_layer(layer, carry):
        for a in range(2):
            await_bytes(layer, a, recv1)
        rows = spread[layer].astype(F32).reshape(ROWS, HALF).astype(BF16)
        for a in range(2):
            half = dot(order[layer, a * 1024 : (a + 1) * 1024, :], rows)
            mid[layer, a] = half.reshape(DEVICES, 8, HALF).astype(BF16)
            send_final(layer, a)

        def patch(a, carry):
            await_bytes(layer, a, recv2)
            result = encode(layer, a)

            @pl.when(layer == 0)
            def _():
                for h in range(2):
                    columns = result[:, h * HALF : (h + 1) * HALF]
                    stage[1, a, h] = columns.reshape(64, 8, HALF).astype(BF16)
                send_spread(1, a)

            @pl.when(layer == LAYERS - 1)
            def _():
                to_local = one_hot(
                    iota((PATCH, PATCH), 0) == local_row(iota((PATCH, PATCH), 1))
                )
                rows = pl.ds(pl.multiple_of(a * PATCH, PATCH), PATCH)
                o_ref[rows, :] = dot(to_local, result.astype(BF16)).astype(BF16)

            return carry

        lax.fori_loop(0, 2, patch, 0)
        return carry

    lax.fori_loop(0, LAYERS, run_layer, 0)
    for layer in range(LAYERS):
        for a in range(2):
            await_bytes(layer, a, send1)
            await_bytes(layer, a, send2)


def per_device(points, moved_to, gains, w_qkv, w_out, w_up, w_down):
    x = points.reshape(2 * PATCH, D)
    moved = jnp.pad(moved_to.reshape(1, 32), ((0, 0), (0, DEVICES - 32)))
    vmem = pl.BlockSpec(memory_space=pltpu.VMEM)
    hbm = pl.BlockSpec(memory_space=pl.ANY)
    dma = pltpu.SemaphoreType.DMA
    out = pl.pallas_call(
        kernel,
        out_shape=jax.ShapeDtypeStruct(x.shape, BF16),
        in_specs=[vmem, vmem, vmem, hbm, hbm, hbm, hbm],
        out_specs=vmem,
        scratch_shapes=[
            pltpu.VMEM(w_qkv.shape, BF16),
            pltpu.VMEM(w_out.shape, BF16),
            pltpu.VMEM(w_up.shape, BF16),
            pltpu.VMEM(w_down.shape, BF16),
            pltpu.VMEM((LAYERS, 2, 2, 64, 8, HALF), BF16),
            pltpu.VMEM((LAYERS, 2, DEVICES, 8, HALF), BF16),
            pltpu.VMEM((LAYERS, 2, DEVICES, 8, HALF), BF16),
            pltpu.VMEM((LAYERS, 2, 2, 64, 8, HALF), BF16),
            pltpu.VMEM((DEVICES, 1, DEVICES), jnp.int32),
            pltpu.VMEM((LAYERS, ROWS, ROWS), BF16),
            pltpu.VMEM((PATCH, 3 * D), BF16),
            pltpu.VMEM((PATCH, HEADS * PATCH), BF16),
            pltpu.VMEM((HEADS * PATCH, 2 * GROUP), BF16),
            pltpu.VMEM((PATCH, D), BF16),
            dma((4,)),
            dma,
            dma((2,)),
            dma((LAYERS, 2)),
            dma((LAYERS, 2)),
            dma((LAYERS, 2)),
            dma((LAYERS, 2)),
        ],
        compiler_params=pltpu.CompilerParams(
            collective_id=0, has_side_effects=True, vmem_limit_bytes=63 * 2**20
        ),
    )(x, moved, gains, w_qkv, w_out, w_up, w_down)
    return out.reshape(points.shape)


def solution(mesh):
    placed = (P(("gx", "gy"), None, None), P(None, None, ("gx", "gy")), P(), P(), P(), P(), P())
    return jax.shard_map(
        per_device,
        mesh=mesh,
        in_specs=placed,
        out_specs=P(("gx", "gy"), None, None),
        check_vma=False,
    )
```

```python
import functools
import math

import jax
import jax.numpy as jnp
from jax import lax
from jax.experimental import pallas as pl
from jax.experimental.pallas import tpu as pltpu
from jax.sharding import PartitionSpec as P

MESH = pl.DeviceIdType.MESH
F32 = jnp.float32
BF16 = jnp.bfloat16

LAYERS = 2
DEVICES = 128
GY = 8
D = 512
FF = 2048
FF_BLOCK = 512
HEAD_DIM = 16
PATCH = 512
GROUP = 128
HEADS = GROUP // HEAD_DIM
HALF = D // 2
ROWS = 2048
SCALE = math.log2(math.e) / math.sqrt(HEAD_DIM)
NT = (((1,), (1,)), ((), ()))
TN = (((0,), (0,)), ((), ()))
TILE = 128
STEP = (0, 1, 3, 2)


def farthest_first():
    found = [
        (bin(v).count("1"), (v * 37 + c) % 64, (STEP[v >> 4], STEP[v >> 2 & 3], STEP[v & 3], c))
        for v in range(64)
        for c in range(2)
        if v or c
    ]
    return [offset for _, _, offset in sorted(found, key=lambda f: (-f[0], f[1]))]


def iota(shape, dim):
    return lax.broadcasted_iota(jnp.int32, shape, dim)


def dot(a, b):
    return jnp.dot(a, b, preferred_element_type=F32)


def one_hot(hit):
    return jnp.where(hit, 1.0, 0.0).astype(BF16)


def row_norm(values, gain):
    center = values - jnp.mean(values, axis=1, keepdims=True)
    spread = jnp.mean(center * center, axis=1, keepdims=True)
    return center * lax.rsqrt(spread + 1e-05) * gain


def local_row(canonical):
    return (canonical % 4) * 128 + (canonical // 8) * 2 + (canonical // 4) % 2


def kernel(
    x_ref, moved_ref, gains_ref, qkv_hbm, out_hbm, up_hbm, down_hbm, o_ref,
    w_qkv, w_out, w_up, w_down, stage, mid, spread, final, table, moved, order,
    w_values, qk, values, probs, attended,
    weight_sem, local_sem, table_sems, send1, recv1, send2, recv2,
):
    row, column = lax.axis_index("gx"), lax.axis_index("gy")
    me = row * GY + column
    ys = [(row // 4 + i) % 4 * 4 for i in range(4)]
    zs = [(row + i) % 4 for i in range(4)]
    xs = [(column // 2 + i) % 4 * 2 for i in range(4)]
    cores = [(column + i) % 2 for i in range(2)]

    def each_peer(body):
        for y, z, x, c in farthest_first():
            there = (ys[y] + zs[z], xs[x] + cores[c])
            body(there[0] * GY + there[1], there)

    weights = []
    for i, (src, dst) in enumerate(
        ((qkv_hbm, w_qkv), (out_hbm, w_out), (up_hbm, w_up), (down_hbm, w_down))
    ):
        copy = pltpu.make_async_copy(src, dst, weight_sem.at[i])
        copy.start()
        weights.append(copy)

    barrier = pltpu.get_barrier_semaphore()
    each_peer(
        lambda p, at: pl.semaphore_signal(barrier, inc=1, device_id=at, device_id_type=MESH)
    )

    to_canonical = one_hot(
        iota((PATCH, PATCH), 1) == local_row(iota((PATCH, PATCH), 0))
    )
    for a in range(2):
        rows = dot(to_canonical, x_ref[a * PATCH : (a + 1) * PATCH, :])
        for h in range(2):
            stage[0, a, h] = rows[:, h * HALF : (h + 1) * HALF].reshape(64, 8, HALF).astype(BF16)
    parts = [moved_ref[l, s : s + 1, :] for l in range(LAYERS) for s in range(2)]
    moved[...] = jnp.concatenate(parts + [jnp.zeros((1, DEVICES - 32), jnp.int32)], axis=1)
    table[me] = moved[...]

    pl.semaphore_wait(barrier, DEVICES - 1)

    def send_table(p, at):
        pltpu.make_async_remote_copy(
            src_ref=moved, dst_ref=table.at[me], send_sem=table_sems.at[0],
            recv_sem=table_sems.at[1], device_id=at, device_id_type=MESH,
        ).start()

    def send_spread(layer, parts):
        def send(p, at):
            for a in parts:
                pltpu.make_async_remote_copy(
                    src_ref=stage.at[layer, a, p % 2, p // 2], dst_ref=spread.at[layer, a, me],
                    send_sem=send1.at[layer, a], recv_sem=recv1.at[layer, a],
                    device_id=at, device_id_type=MESH,
                ).start()

        each_peer(send)
        for a in parts:
            own = pltpu.make_async_copy(
                stage.at[layer, a, me % 2, me // 2], spread.at[layer, a, me], local_sem
            )
            own.start()
            own.wait()

    def send_final(layer, a):
        def send(p, at):
            pltpu.make_async_remote_copy(
                src_ref=mid.at[layer, a, p], dst_ref=final.at[layer, a, me % 2, me // 2],
                send_sem=send2.at[layer, a], recv_sem=recv2.at[layer, a],
                device_id=at, device_id_type=MESH,
            ).start()

        each_peer(send)
        own = pltpu.make_async_copy(
            mid.at[layer, a, me], final.at[layer, a, me % 2, me // 2], local_sem
        )
        own.start()
        own.wait()

    def await_bytes(layer, a, sem):
        part = spread.at[layer, a, 0 : DEVICES - 1]
        pltpu.make_async_copy(part, part, sem.at[layer, a]).wait()

    each_peer(send_table)
    send_spread(0, range(2))

    part = table.at[0 : DEVICES - 1]
    pltpu.make_async_copy(part, part, table_sems.at[1]).wait()
    pltpu.make_async_copy(part, part, table_sems.at[0]).wait()
    moves = table[...].reshape(DEVICES, DEVICES).astype(F32).T[0:32]
    high = jnp.floor(moves * (1 / 32))
    low = (moves - high * 32).astype(BF16)
    high = high.astype(BF16)

    def along(width, owner, slot):
        owners = one_hot(iota((DEVICES, width), 0) == owner(iota((DEVICES, width), 1)))
        hit = iota((32, width), 0) % 8 == slot(iota((32, width), 1))
        both = [jnp.where(hit, dot(v, owners), 0.0) for v in (high, low)]
        return lambda i: [
            jnp.sum(v[i * 8 : (i + 1) * 8], axis=0, keepdims=True) for v in both
        ]

    by_row = along(ROWS, lambda i: i // 8 % DEVICES, lambda i: i // 1024 * 4 + i % 4)
    by_brick = along(1024, lambda i: i // 8, lambda i: i % 8)
    for layer in range(LAYERS):
        first = by_row(2 * layer)
        first = first[0] * 32 + first[1]
        second = by_brick(2 * layer + 1)
        hit = one_hot(iota((1024, ROWS), 0).astype(F32) == first)
        both = jnp.concatenate(second, axis=0).astype(BF16)
        both = dot(jnp.concatenate([both] * 4, axis=0), hit)
        point = (iota((1, ROWS), 1) // 4 % 2).astype(F32)
        code = (both[0:1] * 32 + both[1:2]) * 2 + point
        for r in range(0, ROWS, 512):
            p = iota((512, 1), 0) + r
            want = (p // 8 % DEVICES * 8 + p // 1024 * 4 + p % 4) * 2 + p // 4 % 2
            order[layer, r : r + 512, :] = one_hot(want.astype(F32) == code)

    for copy in weights:
        copy.wait()
    for layer in range(LAYERS):
        w_values[layer] = w_qkv[layer, :, 2 * D :].astype(F32).T.astype(BF16)
    values[:, HEAD_DIM:, :] = jnp.ones((D // HEAD_DIM, HEAD_DIM, PATCH), BF16)
    head_of = iota((PATCH, GROUP), 1) // HEAD_DIM

    def encode(layer, a):
        x = jnp.concatenate(
            [final[layer, a, h].astype(F32).reshape(PATCH, HALF) for h in range(2)], axis=1
        )
        normed = row_norm(x, gains_ref[layer, 0:1, :]).astype(BF16)
        qk[:, 0:D] = (dot(normed, w_qkv[layer, :, 0:D]) * SCALE).astype(BF16)
        qk[:, D:] = dot(normed, w_qkv[layer, :, D : 2 * D]).astype(BF16)
        turned = lax.dot_general(w_values[layer], normed, NT, preferred_element_type=F32)
        values[:, 0:HEAD_DIM, :] = turned.reshape(D // HEAD_DIM, HEAD_DIM, PATCH).astype(BF16)

        def group(g, carry):
            off = pl.multiple_of(g * GROUP, GROUP)
            query = qk[:, pl.ds(off, GROUP)]
            keys = qk[:, pl.ds(pl.multiple_of(D + off, GROUP), GROUP)]
            zero = jnp.zeros((), BF16)

            def mix(h):
                out = dot(values[g * HEADS + h], probs[h])
                rows = pl.ds(pl.multiple_of((g * HEADS + h) * HEAD_DIM, HEAD_DIM), HEAD_DIM)
                attended[rows, :] = (out[0:HEAD_DIM] / out[HEAD_DIM : HEAD_DIM + 1]).astype(BF16)

            for h in range(0, HEADS + 2, 2):
                scores = []
                if h < HEADS:
                    masked = jnp.concatenate(
                        [jnp.where(head_of == h + i, keys, zero) for i in range(2)], axis=0
                    )
                    scores = [
                        lax.dot_general(
                            masked, query[c : c + TILE], NT, preferred_element_type=F32
                        )
                        for c in range(0, PATCH, TILE)
                    ]
                if h >= 2:
                    mix(h - 2)
                    mix(h - 1)
                for i in range(2):
                    for c, tile in enumerate(scores):
                        tile = tile[i * PATCH : (i + 1) * PATCH]
                        peak = jnp.max(tile, axis=0, keepdims=True)
                        columns = slice(c * TILE, (c + 1) * TILE)
                        probs[h + i, :, columns] = jnp.exp2(tile - peak).astype(BF16)
            return carry

        lax.fori_loop(0, D // GROUP, group, 0)
        projected = lax.dot_general(attended[...], w_out[layer], TN, preferred_element_type=F32)
        mixed = (x + projected).astype(BF16).astype(F32)
        inner = row_norm(mixed, gains_ref[layer, 1:2, :]).astype(BF16)
        result = mixed
        for c in range(0, FF, FF_BLOCK):
            up = dot(inner, w_up[layer, :, c : c + FF_BLOCK])
            hidden = (0.5 * up * (1.0 + lax.erf(up * math.sqrt(0.5)))).astype(BF16)
            result = result + dot(hidden, w_down[layer, c : c + FF_BLOCK, :])
        return result

    def run_layer(layer, carry):
        for a in range(2):
            await_bytes(layer, a, recv1)
        rows = spread[layer].astype(F32).reshape(ROWS, HALF).astype(BF16)
        for a in range(2):
            half = dot(order[layer, a * 1024 : (a + 1) * 1024, :], rows)
            mid[layer, a] = half.reshape(DEVICES, 8, HALF).astype(BF16)
            send_final(layer, a)

        def patch(a, carry):
            await_bytes(layer, a, recv2)
            result = encode(layer, a)

            @pl.when(layer == 0)
            def _():
                for h in range(2):
                    columns = result[:, h * HALF : (h + 1) * HALF]
                    stage[1, a, h] = columns.reshape(64, 8, HALF).astype(BF16)
                send_spread(1, (a,))

            @pl.when(layer == LAYERS - 1)
            def _():
                to_local = one_hot(
                    iota((PATCH, PATCH), 0) == local_row(iota((PATCH, PATCH), 1))
                )
                rows = pl.ds(pl.multiple_of(a * PATCH, PATCH), PATCH)
                o_ref[rows, :] = dot(to_local, result.astype(BF16)).astype(BF16)

            return carry

        lax.fori_loop(0, 2, patch, 0)
        return carry

    lax.fori_loop(0, LAYERS, run_layer, 0)
    for layer in range(LAYERS):
        for a in range(2):
            await_bytes(layer, a, send1)
            await_bytes(layer, a, send2)


def per_device(points, moved_to, gains, w_qkv, w_out, w_up, w_down):
    x = points.reshape(2 * PATCH, D)
    vmem = pl.BlockSpec(memory_space=pltpu.VMEM)
    hbm = pl.BlockSpec(memory_space=pl.ANY)
    dma = pltpu.SemaphoreType.DMA
    out = pl.pallas_call(
        kernel,
        out_shape=jax.ShapeDtypeStruct(x.shape, BF16),
        in_specs=[vmem, vmem, vmem, hbm, hbm, hbm, hbm],
        out_specs=vmem,
        scratch_shapes=[
            pltpu.VMEM(w_qkv.shape, BF16),
            pltpu.VMEM(w_out.shape, BF16),
            pltpu.VMEM(w_up.shape, BF16),
            pltpu.VMEM(w_down.shape, BF16),
            pltpu.VMEM((LAYERS, 2, 2, 64, 8, HALF), BF16),
            pltpu.VMEM((LAYERS, 2, DEVICES, 8, HALF), BF16),
            pltpu.VMEM((LAYERS, 2, DEVICES, 8, HALF), BF16),
            pltpu.VMEM((LAYERS, 2, 2, 64, 8, HALF), BF16),
            pltpu.VMEM((DEVICES, 1, DEVICES), jnp.int32),
            pltpu.VMEM((1, DEVICES), jnp.int32),
            pltpu.VMEM((LAYERS, ROWS, ROWS), BF16),
            pltpu.VMEM((LAYERS, D, D), BF16),
            pltpu.VMEM((PATCH, 2 * D), BF16),
            pltpu.VMEM((D // HEAD_DIM, 2 * HEAD_DIM, PATCH), BF16),
            pltpu.VMEM((HEADS, PATCH, PATCH), BF16),
            pltpu.VMEM((D, PATCH), BF16),
            dma((4,)),
            dma,
            dma((2,)),
            dma((LAYERS, 2)),
            dma((LAYERS, 2)),
            dma((LAYERS, 2)),
            dma((LAYERS, 2)),
        ],
        compiler_params=pltpu.CompilerParams(
            collective_id=0, has_side_effects=True, vmem_limit_bytes=63 * 2**20
        ),
    )(x, moved_to, gains, w_qkv, w_out, w_up, w_down)
    return out.reshape(points.shape)


def solution(mesh):
    placed = (P(("gx", "gy"), None, None), P(None, None, ("gx", "gy")), P(), P(), P(), P(), P())
    return jax.shard_map(
        per_device,
        mesh=mesh,
        in_specs=placed,
        out_specs=P(("gx", "gy"), None, None),
        check_vma=False,
    )
```

```python
import functools
import math

import jax
import jax.numpy as jnp
from jax import lax
from jax.experimental import pallas as pl
from jax.experimental.pallas import tpu as pltpu
from jax.sharding import PartitionSpec as P

MESH = pl.DeviceIdType.MESH
F32 = jnp.float32
BF16 = jnp.bfloat16

LAYERS = 2
DEVICES = 128
GY = 8
D = 512
FF = 2048
FF_BLOCK = 512
HEAD_DIM = 16
PATCH = 512
GROUP = 128
HEADS = GROUP // HEAD_DIM
HALF = D // 2
ROWS = 2048
SCALE = math.log2(math.e) / math.sqrt(HEAD_DIM)
NT = (((1,), (1,)), ((), ()))
TN = (((0,), (0,)), ((), ()))
TILE = 128
STEP = (0, 1, 3, 2)


def farthest_first():
    found = [
        (bin(v).count("1"), (v * 37 + c) % 64, (STEP[v >> 4], STEP[v >> 2 & 3], STEP[v & 3], c))
        for v in range(64)
        for c in range(2)
        if v or c
    ]
    return [offset for _, _, offset in sorted(found, key=lambda f: (-f[0], f[1]))]


def iota(shape, dim):
    return lax.broadcasted_iota(jnp.int32, shape, dim)


def dot(a, b):
    return jnp.dot(a, b, preferred_element_type=F32)


def one_hot(hit):
    return jnp.where(hit, 1.0, 0.0).astype(BF16)


def row_norm(values, gain):
    center = values - jnp.mean(values, axis=1, keepdims=True)
    spread = jnp.mean(center * center, axis=1, keepdims=True)
    return center * lax.rsqrt(spread + 1e-05) * gain


def local_row(canonical):
    return (canonical % 4) * 128 + (canonical // 8) * 2 + (canonical // 4) % 2


def kernel(
    x_ref, moved_ref, gains_ref, qkv_hbm, out_hbm, up_hbm, down_hbm, o_ref,
    w_qkv, w_out, w_up, w_down, stage, mid, spread, final, table, moved, order,
    w_values, qk, values, probs, attended,
    weight_sem, local_sem, table_sems, send1, recv1, send2, recv2,
):
    row, column = lax.axis_index("gx"), lax.axis_index("gy")
    me = row * GY + column
    ys = [(row // 4 + i) % 4 * 4 for i in range(4)]
    zs = [(row + i) % 4 for i in range(4)]
    xs = [(column // 2 + i) % 4 * 2 for i in range(4)]
    cores = [(column + i) % 2 for i in range(2)]

    def each_peer(body):
        for y, z, x, c in farthest_first():
            there = (ys[y] + zs[z], xs[x] + cores[c])
            body(there[0] * GY + there[1], there)

    weights = []
    for i, (src, dst) in enumerate(
        ((qkv_hbm, w_qkv), (out_hbm, w_out), (up_hbm, w_up), (down_hbm, w_down))
    ):
        copy = pltpu.make_async_copy(src, dst, weight_sem.at[i])
        copy.start()
        weights.append(copy)

    barrier = pltpu.get_barrier_semaphore()
    each_peer(
        lambda p, at: pl.semaphore_signal(barrier, inc=1, device_id=at, device_id_type=MESH)
    )

    to_canonical = one_hot(
        iota((PATCH, PATCH), 1) == local_row(iota((PATCH, PATCH), 0))
    )
    for a in range(2):
        rows = dot(to_canonical, x_ref[a * PATCH : (a + 1) * PATCH, :])
        for h in range(2):
            stage[0, a, h] = rows[:, h * HALF : (h + 1) * HALF].reshape(64, 8, HALF).astype(BF16)
    parts = [moved_ref[l, s : s + 1, :] for l in range(LAYERS) for s in range(2)]
    moved[...] = jnp.concatenate(parts + [jnp.zeros((1, DEVICES - 32), jnp.int32)], axis=1)
    table[me] = moved[...]

    pl.semaphore_wait(barrier, DEVICES - 1)

    def send_table(p, at):
        pltpu.make_async_remote_copy(
            src_ref=moved, dst_ref=table.at[me], send_sem=table_sems.at[0],
            recv_sem=table_sems.at[1], device_id=at, device_id_type=MESH,
        ).start()

    def send_spread(layer, parts):
        def send(p, at):
            for a in parts:
                pltpu.make_async_remote_copy(
                    src_ref=stage.at[layer, a, p % 2, p // 2], dst_ref=spread.at[layer, a, me],
                    send_sem=send1.at[layer, a], recv_sem=recv1.at[layer, a],
                    device_id=at, device_id_type=MESH,
                ).start()

        each_peer(send)
        for a in parts:
            own = pltpu.make_async_copy(
                stage.at[layer, a, me % 2, me // 2], spread.at[layer, a, me], local_sem
            )
            own.start()
            own.wait()

    def send_final(layer, a):
        def send(p, at):
            pltpu.make_async_remote_copy(
                src_ref=mid.at[layer, a, p], dst_ref=final.at[layer, a, me % 2, me // 2],
                send_sem=send2.at[layer, a], recv_sem=recv2.at[layer, a],
                device_id=at, device_id_type=MESH,
            ).start()

        each_peer(send)
        own = pltpu.make_async_copy(
            mid.at[layer, a, me], final.at[layer, a, me % 2, me // 2], local_sem
        )
        own.start()
        own.wait()

    def await_bytes(layer, a, sem):
        part = spread.at[layer, a, 0 : DEVICES - 1]
        pltpu.make_async_copy(part, part, sem.at[layer, a]).wait()

    each_peer(send_table)
    send_spread(0, range(2))

    part = table.at[0 : DEVICES - 1]
    pltpu.make_async_copy(part, part, table_sems.at[1]).wait()
    pltpu.make_async_copy(part, part, table_sems.at[0]).wait()
    moves = table[...].reshape(DEVICES, DEVICES).astype(F32).T[0:32]
    high = jnp.floor(moves * (1 / 32))
    low = (moves - high * 32).astype(BF16)
    high = high.astype(BF16)

    def along(width, owner, slot):
        owners = one_hot(iota((DEVICES, width), 0) == owner(iota((DEVICES, width), 1)))
        hit = iota((32, width), 0) % 8 == slot(iota((32, width), 1))
        both = [jnp.where(hit, dot(v, owners), 0.0) for v in (high, low)]
        return lambda i: [
            jnp.sum(v[i * 8 : (i + 1) * 8], axis=0, keepdims=True) for v in both
        ]

    by_row = along(ROWS, lambda i: i // 8 % DEVICES, lambda i: i // 1024 * 4 + i % 4)
    by_brick = along(1024, lambda i: i // 8, lambda i: i % 8)

    def build_order(layer):
        first = by_row(2 * layer)
        first = first[0] * 32 + first[1]
        second = by_brick(2 * layer + 1)
        hit = one_hot(iota((1024, ROWS), 0).astype(F32) == first)
        both = jnp.concatenate(second, axis=0).astype(BF16)
        both = dot(jnp.concatenate([both] * 4, axis=0), hit)
        point = (iota((1, ROWS), 1) // 4 % 2).astype(F32)
        code = (both[0:1] * 32 + both[1:2]) * 2 + point
        for r in range(0, ROWS, 512):
            p = iota((512, 1), 0) + r
            want = (p // 8 % DEVICES * 8 + p // 1024 * 4 + p % 4) * 2 + p // 4 % 2
            order[layer, r : r + 512, :] = one_hot(want.astype(F32) == code)

    def turn_weights(layer):
        w_values[layer] = w_qkv[layer, :, 2 * D :].astype(F32).T.astype(BF16)

    for copy in weights:
        copy.wait()
    build_order(0)
    turn_weights(0)
    values[:, HEAD_DIM:, :] = jnp.ones((D // HEAD_DIM, HEAD_DIM, PATCH), BF16)
    head_of = iota((PATCH, GROUP), 1) // HEAD_DIM

    def encode(layer, a):
        x = jnp.concatenate(
            [final[layer, a, h].astype(F32).reshape(PATCH, HALF) for h in range(2)], axis=1
        )
        normed = row_norm(x, gains_ref[layer, 0:1, :]).astype(BF16)
        qk[:, 0:D] = (dot(normed, w_qkv[layer, :, 0:D]) * SCALE).astype(BF16)
        qk[:, D:] = dot(normed, w_qkv[layer, :, D : 2 * D]).astype(BF16)
        turned = lax.dot_general(w_values[layer], normed, NT, preferred_element_type=F32)
        values[:, 0:HEAD_DIM, :] = turned.reshape(D // HEAD_DIM, HEAD_DIM, PATCH).astype(BF16)

        def group(g, carry):
            off = pl.multiple_of(g * GROUP, GROUP)
            query = qk[:, pl.ds(off, GROUP)]
            keys = qk[:, pl.ds(pl.multiple_of(D + off, GROUP), GROUP)]
            zero = jnp.zeros((), BF16)

            def mix(h):
                out = dot(values[g * HEADS + h], probs[h])
                rows = pl.ds(pl.multiple_of((g * HEADS + h) * HEAD_DIM, HEAD_DIM), HEAD_DIM)
                attended[rows, :] = (out[0:HEAD_DIM] / out[HEAD_DIM : HEAD_DIM + 1]).astype(BF16)

            for h in range(HEADS + 1):
                scores = []
                if h < HEADS:
                    masked = jnp.where(head_of == h, keys, zero)
                    scores = [
                        lax.dot_general(
                            masked, query[c : c + TILE], NT, preferred_element_type=F32
                        )
                        for c in range(0, PATCH, TILE)
                    ]
                if h >= 1:
                    mix(h - 1)
                for c in range(0, len(scores), 2):
                    pair = jnp.concatenate(scores[c : c + 2], axis=1)
                    peak = jnp.max(pair, axis=0, keepdims=True)
                    columns = slice(c * TILE, (c + 2) * TILE)
                    probs[h, :, columns] = jnp.exp2(pair - peak).astype(BF16)
            return carry

        lax.fori_loop(0, D // GROUP, group, 0)
        projected = lax.dot_general(attended[...], w_out[layer], TN, preferred_element_type=F32)
        mixed = (x + projected).astype(BF16).astype(F32)
        inner = row_norm(mixed, gains_ref[layer, 1:2, :]).astype(BF16)
        result = mixed
        for c in range(0, FF, FF_BLOCK):
            up = dot(inner, w_up[layer, :, c : c + FF_BLOCK])
            hidden = (0.5 * up * (1.0 + lax.erf(up * math.sqrt(0.5)))).astype(BF16)
            result = result + dot(hidden, w_down[layer, c : c + FF_BLOCK, :])
        return result

    def run_layer(layer, carry):
        halves = []
        for a in range(2):
            await_bytes(layer, a, recv1)
            rows = spread[layer, a].astype(F32).reshape(1024, HALF).astype(BF16)
            if a == 0:
                halves = [
                    dot(order[layer, b * 1024 : (b + 1) * 1024, 0:1024], rows) for b in range(2)
                ]
        for b in range(2):
            half = halves[b] + dot(order[layer, b * 1024 : (b + 1) * 1024, 1024:], rows)
            mid[layer, b] = half.reshape(DEVICES, 8, HALF).astype(BF16)
            if b == 1:
                await_bytes(layer, 0, send2)
            send_final(layer, b)

        @pl.when(layer == 0)
        def _():
            build_order(1)
            turn_weights(1)

        def patch(a, carry):
            await_bytes(layer, a, recv2)
            result = encode(layer, a)

            @pl.when(layer == 0)
            def _():
                for h in range(2):
                    columns = result[:, h * HALF : (h + 1) * HALF]
                    stage[1, a, h] = columns.reshape(64, 8, HALF).astype(BF16)
                send_spread(1, (a,))

            @pl.when(layer == LAYERS - 1)
            def _():
                o_ref[pl.ds(pl.multiple_of(a * PATCH, PATCH), PATCH), :] = result.astype(BF16)

            return carry

        lax.fori_loop(0, 2, patch, 0)
        return carry

    lax.fori_loop(0, LAYERS, run_layer, 0)
    for layer in range(LAYERS):
        for a in range(2):
            await_bytes(layer, a, send1)
        await_bytes(layer, 1, send2)


def to_local_order(x_ref, o_ref):
    hit = iota((PATCH, PATCH), 0) == local_row(iota((PATCH, PATCH), 1))
    o_ref[...] = dot(one_hot(hit), x_ref[...]).astype(BF16)


def per_device(points, moved_to, gains, w_qkv, w_out, w_up, w_down):
    x = points.reshape(2 * PATCH, D)
    vmem = pl.BlockSpec(memory_space=pltpu.VMEM)
    hbm = pl.BlockSpec(memory_space=pl.ANY)
    dma = pltpu.SemaphoreType.DMA
    out = pl.pallas_call(
        kernel,
        out_shape=jax.ShapeDtypeStruct(x.shape, BF16),
        in_specs=[vmem, vmem, vmem, hbm, hbm, hbm, hbm],
        out_specs=vmem,
        scratch_shapes=[
            pltpu.VMEM(w_qkv.shape, BF16),
            pltpu.VMEM(w_out.shape, BF16),
            pltpu.VMEM(w_up.shape, BF16),
            pltpu.VMEM(w_down.shape, BF16),
            pltpu.VMEM((LAYERS, 2, 2, 64, 8, HALF), BF16),
            pltpu.VMEM((LAYERS, 2, DEVICES, 8, HALF), BF16),
            pltpu.VMEM((LAYERS, 2, DEVICES, 8, HALF), BF16),
            pltpu.VMEM((LAYERS, 2, 2, 64, 8, HALF), BF16),
            pltpu.VMEM((DEVICES, 1, DEVICES), jnp.int32),
            pltpu.VMEM((1, DEVICES), jnp.int32),
            pltpu.VMEM((LAYERS, ROWS, ROWS), BF16),
            pltpu.VMEM((LAYERS, D, D), BF16),
            pltpu.VMEM((PATCH, 2 * D), BF16),
            pltpu.VMEM((D // HEAD_DIM, 2 * HEAD_DIM, PATCH), BF16),
            pltpu.VMEM((HEADS, PATCH, PATCH), BF16),
            pltpu.VMEM((D, PATCH), BF16),
            dma((4,)),
            dma,
            dma((2,)),
            dma((LAYERS, 2)),
            dma((LAYERS, 2)),
            dma((LAYERS, 2)),
            dma((LAYERS, 2)),
        ],
        compiler_params=pltpu.CompilerParams(
            collective_id=0, has_side_effects=True, vmem_limit_bytes=63 * 2**20
        ),
    )(x, moved_to, gains, w_qkv, w_out, w_up, w_down)
    half = pl.BlockSpec((PATCH, D), lambda a: (a, 0))
    out = pl.pallas_call(
        to_local_order,
        grid=(2,),
        in_specs=[half],
        out_specs=half,
        out_shape=jax.ShapeDtypeStruct(x.shape, BF16),
    )(out)
    return out.reshape(points.shape)


def solution(mesh):
    placed = (P(("gx", "gy"), None, None), P(None, None, ("gx", "gy")), P(), P(), P(), P(), P())
    return jax.shard_map(
        per_device,
        mesh=mesh,
        in_specs=placed,
        out_specs=P(("gx", "gy"), None, None),
        check_vma=False,
    )
```

```python
import functools
import math

import jax
import jax.numpy as jnp
from jax import lax
from jax.experimental import pallas as pl
from jax.experimental.pallas import tpu as pltpu
from jax.sharding import PartitionSpec as P

MESH = pl.DeviceIdType.MESH
F32 = jnp.float32
BF16 = jnp.bfloat16

LAYERS = 2
DEVICES = 128
GY = 8
D = 512
FF = 2048
FF_BLOCK = 512
HEAD_DIM = 16
PATCH = 512
GROUP = 128
HEADS = GROUP // HEAD_DIM
HALF = D // 2
ROWS = 2048
SCALE = math.log2(math.e) / math.sqrt(HEAD_DIM)
NT = (((1,), (1,)), ((), ()))
TN = (((0,), (0,)), ((), ()))
TILE = 128
JOINED = 4
STEP = (0, 1, 3, 2)


def farthest_first():
    found = [
        (bin(v).count("1"), (v * 37 + c) % 64, (STEP[v >> 4], STEP[v >> 2 & 3], STEP[v & 3], c))
        for v in range(64)
        for c in range(2)
        if v or c
    ]
    return [offset for _, _, offset in sorted(found, key=lambda f: (-f[0], f[1]))]


def iota(shape, dim):
    return lax.broadcasted_iota(jnp.int32, shape, dim)


def dot(a, b):
    return jnp.dot(a, b, preferred_element_type=F32)


def one_hot(hit):
    return jnp.where(hit, 1.0, 0.0).astype(BF16)


def row_norm(values, gain):
    center = values - jnp.mean(values, axis=1, keepdims=True)
    spread = jnp.mean(center * center, axis=1, keepdims=True)
    return center * lax.rsqrt(spread + 1e-05) * gain


def local_row(canonical):
    return (canonical % 4) * 128 + (canonical // 8) * 2 + (canonical // 4) % 2


def kernel(
    x_ref, moved_ref, gains_ref, qkv_hbm, out_hbm, up_hbm, down_hbm, o_ref,
    w_qkv, w_out, w_up, w_down, stage, mid, spread, final, table, moved, order,
    w_values, qk, values, probs, attended,
    weight_sem, local_sem, table_sems, send1, recv1, send2, recv2,
):
    row, column = lax.axis_index("gx"), lax.axis_index("gy")
    me = row * GY + column
    ys = [(row // 4 + i) % 4 * 4 for i in range(4)]
    zs = [(row + i) % 4 for i in range(4)]
    xs = [(column // 2 + i) % 4 * 2 for i in range(4)]
    cores = [(column + i) % 2 for i in range(2)]

    def each_peer(body):
        for y, z, x, c in farthest_first():
            there = (ys[y] + zs[z], xs[x] + cores[c])
            body(there[0] * GY + there[1], there)

    weights = []
    for i, (src, dst) in enumerate(
        ((qkv_hbm, w_qkv), (out_hbm, w_out), (up_hbm, w_up), (down_hbm, w_down))
    ):
        copy = pltpu.make_async_copy(src, dst, weight_sem.at[i])
        copy.start()
        weights.append(copy)

    barrier = pltpu.get_barrier_semaphore()
    each_peer(
        lambda p, at: pl.semaphore_signal(barrier, inc=1, device_id=at, device_id_type=MESH)
    )

    to_canonical = one_hot(
        iota((PATCH, PATCH), 1) == local_row(iota((PATCH, PATCH), 0))
    )
    for a in range(2):
        rows = dot(to_canonical, x_ref[a * PATCH : (a + 1) * PATCH, :])
        for h in range(2):
            stage[0, a, h] = rows[:, h * HALF : (h + 1) * HALF].reshape(64, 8, HALF).astype(BF16)
    parts = [moved_ref[l, s : s + 1, :] for l in range(LAYERS) for s in range(2)]
    moved[...] = jnp.concatenate(parts + [jnp.zeros((1, DEVICES - 32), jnp.int32)], axis=1)
    table[me] = moved[...]

    pl.semaphore_wait(barrier, DEVICES - 1)

    def send_table(p, at):
        pltpu.make_async_remote_copy(
            src_ref=moved, dst_ref=table.at[me], send_sem=table_sems.at[0],
            recv_sem=table_sems.at[1], device_id=at, device_id_type=MESH,
        ).start()

    def send_spread(layer, parts):
        def send(p, at):
            for a in parts:
                pltpu.make_async_remote_copy(
                    src_ref=stage.at[layer, a, p % 2, p // 2], dst_ref=spread.at[layer, a, me],
                    send_sem=send1.at[layer, a], recv_sem=recv1.at[layer, a],
                    device_id=at, device_id_type=MESH,
                ).start()

        each_peer(send)
        for a in parts:
            own = pltpu.make_async_copy(
                stage.at[layer, a, me % 2, me // 2], spread.at[layer, a, me], local_sem
            )
            own.start()
            own.wait()

    def send_final(layer, a):
        def send(p, at):
            pltpu.make_async_remote_copy(
                src_ref=mid.at[layer, a, p], dst_ref=final.at[layer, a, me % 2, me // 2],
                send_sem=send2.at[layer, a], recv_sem=recv2.at[layer, a],
                device_id=at, device_id_type=MESH,
            ).start()

        each_peer(send)
        own = pltpu.make_async_copy(
            mid.at[layer, a, me], final.at[layer, a, me % 2, me // 2], local_sem
        )
        own.start()
        own.wait()

    def await_bytes(layer, a, sem):
        part = spread.at[layer, a, 0 : DEVICES - 1]
        pltpu.make_async_copy(part, part, sem.at[layer, a]).wait()

    each_peer(send_table)
    send_spread(0, range(2))

    part = table.at[0 : DEVICES - 1]
    pltpu.make_async_copy(part, part, table_sems.at[1]).wait()
    pltpu.make_async_copy(part, part, table_sems.at[0]).wait()
    moves = table[...].reshape(DEVICES, DEVICES).astype(F32).T[0:32]
    high = jnp.floor(moves * (1 / 32))
    low = (moves - high * 32).astype(BF16)
    high = high.astype(BF16)

    def along(width, owner, slot):
        owners = one_hot(iota((DEVICES, width), 0) == owner(iota((DEVICES, width), 1)))
        hit = iota((32, width), 0) % 8 == slot(iota((32, width), 1))
        both = [jnp.where(hit, dot(v, owners), 0.0) for v in (high, low)]
        return lambda i: [
            jnp.sum(v[i * 8 : (i + 1) * 8], axis=0, keepdims=True) for v in both
        ]

    by_row = along(ROWS, lambda i: i // 8 % DEVICES, lambda i: i // 1024 * 4 + i % 4)
    by_brick = along(1024, lambda i: i // 8, lambda i: i % 8)

    def build_order(layer):
        first = by_row(2 * layer)
        first = first[0] * 32 + first[1]
        second = by_brick(2 * layer + 1)
        hit = one_hot(iota((1024, ROWS), 0).astype(F32) == first)
        both = jnp.concatenate(second, axis=0).astype(BF16)
        both = dot(jnp.concatenate([both] * 4, axis=0), hit)
        point = (iota((1, ROWS), 1) // 4 % 2).astype(F32)
        code = (both[0:1] * 32 + both[1:2]) * 2 + point
        for r in range(0, ROWS, 512):
            p = iota((512, 1), 0) + r
            want = (p // 8 % DEVICES * 8 + p // 1024 * 4 + p % 4) * 2 + p // 4 % 2
            order[layer, r : r + 512, :] = one_hot(want.astype(F32) == code)

    def turn_weights(layer):
        w_values[layer] = w_qkv[layer, :, 2 * D :].astype(F32).T.astype(BF16)

    for copy in weights:
        copy.wait()
    build_order(0)
    turn_weights(0)
    values[:, HEAD_DIM:, :] = jnp.ones((D // HEAD_DIM, HEAD_DIM, PATCH), BF16)
    head_of = iota((PATCH, GROUP), 1) // HEAD_DIM

    def encode(layer, a):
        x = jnp.concatenate(
            [final[layer, a, h].astype(F32).reshape(PATCH, HALF) for h in range(2)], axis=1
        )
        normed = row_norm(x, gains_ref[layer, 0:1, :]).astype(BF16)
        qk[:, 0:D] = (dot(normed, w_qkv[layer, :, 0:D]) * SCALE).astype(BF16)
        qk[:, D:] = dot(normed, w_qkv[layer, :, D : 2 * D]).astype(BF16)
        turned = lax.dot_general(w_values[layer], normed, NT, preferred_element_type=F32)
        values[:, 0:HEAD_DIM, :] = turned.reshape(D // HEAD_DIM, HEAD_DIM, PATCH).astype(BF16)

        def group(g, carry):
            zero = jnp.zeros((), BF16)

            def mix(h):
                head = g * (JOINED * HEADS) + h
                out = dot(values[head], probs[h % HEADS])
                rows = pl.ds(pl.multiple_of(head * HEAD_DIM, HEAD_DIM), HEAD_DIM)
                attended[rows, :] = (out[0:HEAD_DIM] / out[HEAD_DIM : HEAD_DIM + 1]).astype(BF16)

            for h in range(JOINED * HEADS + 1):
                scores = []
                if h < JOINED * HEADS:
                    off = pl.multiple_of((g * JOINED + h // HEADS) * GROUP, GROUP)
                    query = qk[:, pl.ds(off, GROUP)]
                    keys = qk[:, pl.ds(pl.multiple_of(D + off, GROUP), GROUP)]
                    masked = jnp.where(head_of == h % HEADS, keys, zero)
                    scores = [
                        lax.dot_general(
                            masked, query[c : c + TILE], NT, preferred_element_type=F32
                        )
                        for c in range(0, PATCH, TILE)
                    ]
                if h >= 1:
                    mix(h - 1)
                for c in range(0, len(scores), 2):
                    pair = jnp.concatenate(scores[c : c + 2], axis=1)
                    peak = jnp.max(pair, axis=0, keepdims=True)
                    columns = slice(c * TILE, (c + 2) * TILE)
                    probs[h % HEADS, :, columns] = jnp.exp2(pair - peak).astype(BF16)
            return carry

        lax.fori_loop(0, D // GROUP // JOINED, group, 0)
        projected = lax.dot_general(attended[...], w_out[layer], TN, preferred_element_type=F32)
        mixed = (x + projected).astype(BF16).astype(F32)
        inner = row_norm(mixed, gains_ref[layer, 1:2, :]).astype(BF16)
        result = mixed
        for c in range(0, FF, FF_BLOCK):
            up = dot(inner, w_up[layer, :, c : c + FF_BLOCK])
            hidden = (0.5 * up * (1.0 + lax.erf(up * math.sqrt(0.5)))).astype(BF16)
            result = result + dot(hidden, w_down[layer, c : c + FF_BLOCK, :])
        return result

    def run_layer(layer, carry):
        halves = []
        for a in range(2):
            await_bytes(layer, a, recv1)
            rows = spread[layer, a].astype(F32).reshape(1024, HALF).astype(BF16)
            if a == 0:
                halves = [
                    dot(order[layer, b * 1024 : (b + 1) * 1024, 0:1024], rows) for b in range(2)
                ]
        for b in range(2):
            half = halves[b] + dot(order[layer, b * 1024 : (b + 1) * 1024, 1024:], rows)
            mid[layer, b] = half.reshape(DEVICES, 8, HALF).astype(BF16)
            if b == 1:
                await_bytes(layer, 0, send2)
            send_final(layer, b)

        @pl.when(layer == 0)
        def _():
            build_order(1)
            turn_weights(1)

        def patch(a, carry):
            await_bytes(layer, a, recv2)
            result = encode(layer, a)

            @pl.when(layer == 0)
            def _():
                for h in range(2):
                    columns = result[:, h * HALF : (h + 1) * HALF]
                    stage[1, a, h] = columns.reshape(64, 8, HALF).astype(BF16)
                send_spread(1, (a,))

            @pl.when(layer == LAYERS - 1)
            def _():
                o_ref[pl.ds(pl.multiple_of(a * PATCH, PATCH), PATCH), :] = result.astype(BF16)

            return carry

        lax.fori_loop(0, 2, patch, 0)
        return carry

    lax.fori_loop(0, LAYERS, run_layer, 0)
    for layer in range(LAYERS):
        for a in range(2):
            await_bytes(layer, a, send1)
        await_bytes(layer, 1, send2)


def to_local_order(x_ref, o_ref):
    hit = iota((PATCH, PATCH), 0) == local_row(iota((PATCH, PATCH), 1))
    o_ref[...] = dot(one_hot(hit), x_ref[...]).astype(BF16)


def per_device(points, moved_to, gains, w_qkv, w_out, w_up, w_down):
    x = points.reshape(2 * PATCH, D)
    vmem = pl.BlockSpec(memory_space=pltpu.VMEM)
    hbm = pl.BlockSpec(memory_space=pl.ANY)
    dma = pltpu.SemaphoreType.DMA
    out = pl.pallas_call(
        kernel,
        out_shape=jax.ShapeDtypeStruct(x.shape, BF16),
        in_specs=[vmem, vmem, vmem, hbm, hbm, hbm, hbm],
        out_specs=vmem,
        scratch_shapes=[
            pltpu.VMEM(w_qkv.shape, BF16),
            pltpu.VMEM(w_out.shape, BF16),
            pltpu.VMEM(w_up.shape, BF16),
            pltpu.VMEM(w_down.shape, BF16),
            pltpu.VMEM((LAYERS, 2, 2, 64, 8, HALF), BF16),
            pltpu.VMEM((LAYERS, 2, DEVICES, 8, HALF), BF16),
            pltpu.VMEM((LAYERS, 2, DEVICES, 8, HALF), BF16),
            pltpu.VMEM((LAYERS, 2, 2, 64, 8, HALF), BF16),
            pltpu.VMEM((DEVICES, 1, DEVICES), jnp.int32),
            pltpu.VMEM((1, DEVICES), jnp.int32),
            pltpu.VMEM((LAYERS, ROWS, ROWS), BF16),
            pltpu.VMEM((LAYERS, D, D), BF16),
            pltpu.VMEM((PATCH, 2 * D), BF16),
            pltpu.VMEM((D // HEAD_DIM, 2 * HEAD_DIM, PATCH), BF16),
            pltpu.VMEM((HEADS, PATCH, PATCH), BF16),
            pltpu.VMEM((D, PATCH), BF16),
            dma((4,)),
            dma,
            dma((2,)),
            dma((LAYERS, 2)),
            dma((LAYERS, 2)),
            dma((LAYERS, 2)),
            dma((LAYERS, 2)),
        ],
        compiler_params=pltpu.CompilerParams(
            collective_id=0, has_side_effects=True, vmem_limit_bytes=63 * 2**20
        ),
    )(x, moved_to, gains, w_qkv, w_out, w_up, w_down)
    half = pl.BlockSpec((PATCH, D), lambda a: (a, 0))
    out = pl.pallas_call(
        to_local_order,
        grid=(2,),
        in_specs=[half],
        out_specs=half,
        out_shape=jax.ShapeDtypeStruct(x.shape, BF16),
    )(out)
    return out.reshape(points.shape)


def solution(mesh):
    placed = (P(("gx", "gy"), None, None), P(None, None, ("gx", "gy")), P(), P(), P(), P(), P())
    return jax.shard_map(
        per_device,
        mesh=mesh,
        in_specs=placed,
        out_specs=P(("gx", "gy"), None, None),
        check_vma=False,
    )
```

```python
import functools
import math

import jax
import jax.numpy as jnp
from jax import lax
from jax.experimental import pallas as pl
from jax.experimental.pallas import tpu as pltpu
from jax.sharding import PartitionSpec as P

MESH = pl.DeviceIdType.MESH
F32 = jnp.float32
BF16 = jnp.bfloat16

LAYERS = 2
DEVICES = 128
GY = 8
D = 512
FF = 2048
FF_BLOCK = 512
HEAD_DIM = 16
PATCH = 512
GROUP = 128
HEADS = GROUP // HEAD_DIM
HALF = D // 2
ROWS = 2048
SCALE = math.log2(math.e) / math.sqrt(HEAD_DIM)
NT = (((1,), (1,)), ((), ()))
TN = (((0,), (0,)), ((), ()))
TILE = 128
JOINED = 4
STEP = (0, 1, 3, 2)


def farthest_first():
    found = [
        (bin(v).count("1"), (v * 37 + c) % 64, (STEP[v >> 4], STEP[v >> 2 & 3], STEP[v & 3], c))
        for v in range(64)
        for c in range(2)
        if v or c
    ]
    return [offset for _, _, offset in sorted(found, key=lambda f: (-f[0], f[1]))]


def iota(shape, dim):
    return lax.broadcasted_iota(jnp.int32, shape, dim)


def dot(a, b):
    return jnp.dot(a, b, preferred_element_type=F32)


def one_hot(hit):
    return jnp.where(hit, 1.0, 0.0).astype(BF16)


def row_norm(values, gain):
    center = values - jnp.mean(values, axis=1, keepdims=True)
    spread = jnp.mean(center * center, axis=1, keepdims=True)
    return center * lax.rsqrt(spread + 1e-05) * gain


def local_row(canonical):
    return (canonical % 4) * 128 + (canonical // 8) * 2 + (canonical // 4) % 2


def kernel(
    x_ref, moved_ref, gains_ref, qkv_hbm, out_hbm, up_hbm, down_hbm, o_ref,
    w_qkv, w_out, w_up, w_down, stage, mid, spread, final, table, moved, order,
    w_values, qk, values, probs, attended,
    weight_sem, local_sem, table_sems, send1, recv1, send2, recv2,
):
    row, column = lax.axis_index("gx"), lax.axis_index("gy")
    me = row * GY + column
    ys = [(row // 4 + i) % 4 * 4 for i in range(4)]
    zs = [(row + i) % 4 for i in range(4)]
    xs = [(column // 2 + i) % 4 * 2 for i in range(4)]
    cores = [(column + i) % 2 for i in range(2)]

    def each_peer(body):
        for y, z, x, c in farthest_first():
            there = (ys[y] + zs[z], xs[x] + cores[c])
            body(there[0] * GY + there[1], there)

    weights = []
    for i, (src, dst) in enumerate(
        ((qkv_hbm, w_qkv), (out_hbm, w_out), (up_hbm, w_up), (down_hbm, w_down))
    ):
        copy = pltpu.make_async_copy(src, dst, weight_sem.at[i])
        copy.start()
        weights.append(copy)

    barrier = pltpu.get_barrier_semaphore()
    each_peer(
        lambda p, at: pl.semaphore_signal(barrier, inc=1, device_id=at, device_id_type=MESH)
    )

    to_canonical = one_hot(
        iota((PATCH, PATCH), 1) == local_row(iota((PATCH, PATCH), 0))
    )
    for a in range(2):
        rows = dot(to_canonical, x_ref[a * PATCH : (a + 1) * PATCH, :])
        for h in range(2):
            stage[0, a, h] = rows[:, h * HALF : (h + 1) * HALF].reshape(64, 8, HALF).astype(BF16)
    parts = [moved_ref[l, s : s + 1, :] for l in range(LAYERS) for s in range(2)]
    moved[...] = jnp.concatenate(parts + [jnp.zeros((1, DEVICES - 32), jnp.int32)], axis=1)
    table[me] = moved[...]

    pl.semaphore_wait(barrier, DEVICES - 1)

    def send_table(p, at):
        pltpu.make_async_remote_copy(
            src_ref=moved, dst_ref=table.at[me], send_sem=table_sems.at[0],
            recv_sem=table_sems.at[1], device_id=at, device_id_type=MESH,
        ).start()

    def send_spread(layer, parts):
        def send(p, at):
            for a in parts:
                pltpu.make_async_remote_copy(
                    src_ref=stage.at[layer, a, p % 2, p // 2], dst_ref=spread.at[layer, a, me],
                    send_sem=send1.at[layer, a], recv_sem=recv1.at[layer, a],
                    device_id=at, device_id_type=MESH,
                ).start()

        each_peer(send)
        for a in parts:
            own = pltpu.make_async_copy(
                stage.at[layer, a, me % 2, me // 2], spread.at[layer, a, me], local_sem
            )
            own.start()
            own.wait()

    def send_final(layer, a):
        def send(p, at):
            pltpu.make_async_remote_copy(
                src_ref=mid.at[layer, a, p], dst_ref=final.at[layer, a, me % 2, me // 2],
                send_sem=send2.at[layer, a], recv_sem=recv2.at[layer, a],
                device_id=at, device_id_type=MESH,
            ).start()

        each_peer(send)
        own = pltpu.make_async_copy(
            mid.at[layer, a, me], final.at[layer, a, me % 2, me // 2], local_sem
        )
        own.start()
        own.wait()

    def await_bytes(layer, a, sem):
        part = spread.at[layer, a, 0 : DEVICES - 1]
        pltpu.make_async_copy(part, part, sem.at[layer, a]).wait()

    each_peer(send_table)
    send_spread(0, range(2))

    part = table.at[0 : DEVICES - 1]
    pltpu.make_async_copy(part, part, table_sems.at[1]).wait()
    pltpu.make_async_copy(part, part, table_sems.at[0]).wait()
    moves = table[...].reshape(DEVICES, DEVICES).astype(F32).T[0:32]
    high = jnp.floor(moves * (1 / 32))
    low = (moves - high * 32).astype(BF16)
    high = high.astype(BF16)

    def along(width, owner, slot):
        owners = one_hot(iota((DEVICES, width), 0) == owner(iota((DEVICES, width), 1)))
        hit = iota((32, width), 0) % 8 == slot(iota((32, width), 1))
        both = [jnp.where(hit, dot(v, owners), 0.0) for v in (high, low)]
        return lambda i: [
            jnp.sum(v[i * 8 : (i + 1) * 8], axis=0, keepdims=True) for v in both
        ]

    by_row = along(ROWS, lambda i: i // 8 % DEVICES, lambda i: i // 1024 * 4 + i % 4)
    by_brick = along(1024, lambda i: i // 8, lambda i: i % 8)

    def build_order(layer):
        first = by_row(2 * layer)
        first = first[0] * 32 + first[1]
        second = by_brick(2 * layer + 1)
        hit = one_hot(iota((1024, ROWS), 0).astype(F32) == first)
        both = jnp.concatenate(second, axis=0).astype(BF16)
        both = dot(jnp.concatenate([both] * 4, axis=0), hit)
        point = (iota((1, ROWS), 1) // 4 % 2).astype(F32)
        code = (both[0:1] * 32 + both[1:2]) * 2 + point
        for r in range(0, ROWS, 512):
            p = iota((512, 1), 0) + r
            want = (p // 8 % DEVICES * 8 + p // 1024 * 4 + p % 4) * 2 + p // 4 % 2
            order[layer, r : r + 512, :] = one_hot(want.astype(F32) == code)

    def turn_weights(layer):
        w_values[layer] = w_qkv[layer, :, 2 * D :].astype(F32).T.astype(BF16)

    for copy in weights:
        copy.wait()
    build_order(0)
    turn_weights(0)
    values[:, HEAD_DIM:, :] = jnp.ones((D // HEAD_DIM, HEAD_DIM, PATCH), BF16)
    head_of = iota((PATCH, GROUP), 1) // HEAD_DIM

    def encode(layer, a):
        x = jnp.concatenate(
            [final[layer, a, h].astype(F32).reshape(PATCH, HALF) for h in range(2)], axis=1
        )
        normed = row_norm(x, gains_ref[layer, 0:1, :]).astype(BF16)
        qk[:, 0:D] = (dot(normed, w_qkv[layer, :, 0:D]) * SCALE).astype(BF16)
        qk[:, D:] = dot(normed, w_qkv[layer, :, D : 2 * D]).astype(BF16)
        turned = lax.dot_general(w_values[layer], normed, NT, preferred_element_type=F32)
        values[:, 0:HEAD_DIM, :] = turned.reshape(D // HEAD_DIM, HEAD_DIM, PATCH).astype(BF16)

        def group(g, carry):
            zero = jnp.zeros((), BF16)

            def mix(h):
                head = g * (JOINED * HEADS) + h
                out = dot(values[head], probs[h % HEADS])
                rows = pl.ds(pl.multiple_of(head * HEAD_DIM, HEAD_DIM), HEAD_DIM)
                attended[rows, :] = (out[0:HEAD_DIM] / out[HEAD_DIM : HEAD_DIM + 1]).astype(BF16)

            for h in range(JOINED * HEADS + 1):
                scores = []
                if h < JOINED * HEADS:
                    off = pl.multiple_of((g * JOINED + h // HEADS) * GROUP, GROUP)
                    query = qk[:, pl.ds(off, GROUP)]
                    keys = qk[:, pl.ds(pl.multiple_of(D + off, GROUP), GROUP)]
                    masked = jnp.where(head_of == h % HEADS, keys, zero)
                    scores = [
                        lax.dot_general(
                            masked, query[c : c + TILE], NT, preferred_element_type=F32
                        )
                        for c in range(0, PATCH, TILE)
                    ]
                if h >= 1:
                    mix(h - 1)
                for c in range(0, len(scores), 2):
                    pair = jnp.concatenate(scores[c : c + 2], axis=1)
                    peak = jnp.max(pair, axis=0, keepdims=True)
                    columns = slice(c * TILE, (c + 2) * TILE)
                    probs[h % HEADS, :, columns] = jnp.exp2(pair - peak).astype(BF16)
            return carry

        lax.fori_loop(0, D // GROUP // JOINED, group, 0)
        projected = lax.dot_general(attended[...], w_out[layer], TN, preferred_element_type=F32)
        mixed = (x + projected).astype(BF16).astype(F32)
        inner = row_norm(mixed, gains_ref[layer, 1:2, :]).astype(BF16)
        result = mixed
        for c in range(0, FF, FF_BLOCK):
            up = dot(inner, w_up[layer, :, c : c + FF_BLOCK])
            hidden = (0.5 * up * (1.0 + lax.erf(up * math.sqrt(0.5)))).astype(BF16)
            result = result + dot(hidden, w_down[layer, c : c + FF_BLOCK, :])
        return result

    def run_layer(layer, carry):
        halves = []
        for a in range(2):
            await_bytes(layer, a, recv1)
            rows = spread[layer, a].astype(F32).reshape(1024, HALF).astype(BF16)
            if a == 0:
                halves = [
                    dot(order[layer, b * 1024 : (b + 1) * 1024, 0:1024], rows) for b in range(2)
                ]
        for b in range(2):
            half = halves[b] + dot(order[layer, b * 1024 : (b + 1) * 1024, 1024:], rows)
            mid[layer, b] = half.reshape(DEVICES, 8, HALF).astype(BF16)
            if b == 0:
                send_final(layer, 0)

        @pl.when(layer == 0)
        def _():
            build_order(1)
            turn_weights(1)

        await_bytes(layer, 0, send2)
        await_bytes(layer, 0, recv2)
        send_final(layer, 1)

        def patch(a, carry):
            @pl.when(a == 1)
            def _():
                await_bytes(layer, 1, recv2)

            result = encode(layer, a)

            @pl.when(layer == 0)
            def _():
                for h in range(2):
                    columns = result[:, h * HALF : (h + 1) * HALF]
                    stage[1, a, h] = columns.reshape(64, 8, HALF).astype(BF16)
                send_spread(1, (a,))

            @pl.when(layer == LAYERS - 1)
            def _():
                o_ref[pl.ds(pl.multiple_of(a * PATCH, PATCH), PATCH), :] = result.astype(BF16)

            return carry

        lax.fori_loop(0, 2, patch, 0)
        return carry

    lax.fori_loop(0, LAYERS, run_layer, 0)
    for layer in range(LAYERS):
        for a in range(2):
            await_bytes(layer, a, send1)
        await_bytes(layer, 1, send2)


def to_local_order(x_ref, o_ref):
    hit = iota((PATCH, PATCH), 0) == local_row(iota((PATCH, PATCH), 1))
    o_ref[...] = dot(one_hot(hit), x_ref[...]).astype(BF16)


def per_device(points, moved_to, gains, w_qkv, w_out, w_up, w_down):
    x = points.reshape(2 * PATCH, D)
    vmem = pl.BlockSpec(memory_space=pltpu.VMEM)
    hbm = pl.BlockSpec(memory_space=pl.ANY)
    dma = pltpu.SemaphoreType.DMA
    out = pl.pallas_call(
        kernel,
        out_shape=jax.ShapeDtypeStruct(x.shape, BF16),
        in_specs=[vmem, vmem, vmem, hbm, hbm, hbm, hbm],
        out_specs=vmem,
        scratch_shapes=[
            pltpu.VMEM(w_qkv.shape, BF16),
            pltpu.VMEM(w_out.shape, BF16),
            pltpu.VMEM(w_up.shape, BF16),
            pltpu.VMEM(w_down.shape, BF16),
            pltpu.VMEM((LAYERS, 2, 2, 64, 8, HALF), BF16),
            pltpu.VMEM((LAYERS, 2, DEVICES, 8, HALF), BF16),
            pltpu.VMEM((LAYERS, 2, DEVICES, 8, HALF), BF16),
            pltpu.VMEM((LAYERS, 2, 2, 64, 8, HALF), BF16),
            pltpu.VMEM((DEVICES, 1, DEVICES), jnp.int32),
            pltpu.VMEM((1, DEVICES), jnp.int32),
            pltpu.VMEM((LAYERS, ROWS, ROWS), BF16),
            pltpu.VMEM((LAYERS, D, D), BF16),
            pltpu.VMEM((PATCH, 2 * D), BF16),
            pltpu.VMEM((D // HEAD_DIM, 2 * HEAD_DIM, PATCH), BF16),
            pltpu.VMEM((HEADS, PATCH, PATCH), BF16),
            pltpu.VMEM((D, PATCH), BF16),
            dma((4,)),
            dma,
            dma((2,)),
            dma((LAYERS, 2)),
            dma((LAYERS, 2)),
            dma((LAYERS, 2)),
            dma((LAYERS, 2)),
        ],
        compiler_params=pltpu.CompilerParams(
            collective_id=0, has_side_effects=True, vmem_limit_bytes=63 * 2**20
        ),
    )(x, moved_to, gains, w_qkv, w_out, w_up, w_down)
    half = pl.BlockSpec((PATCH, D), lambda a: (a, 0))
    out = pl.pallas_call(
        to_local_order,
        grid=(2,),
        in_specs=[half],
        out_specs=half,
        out_shape=jax.ShapeDtypeStruct(x.shape, BF16),
    )(out)
    return out.reshape(points.shape)


def solution(mesh):
    placed = (P(("gx", "gy"), None, None), P(None, None, ("gx", "gy")), P(), P(), P(), P(), P())
    return jax.shard_map(
        per_device,
        mesh=mesh,
        in_specs=placed,
        out_specs=P(("gx", "gy"), None, None),
        check_vma=False,
    )
```
